256 devices in a mesh: src: 16 (over y_lo, x, core), tgt: 16 (over z, y_hi).
Axes of the slice: x: 4, y: 4 (y_hi: 2, y_lo: 2; y = y_hi * 2 + y_lo), z: 8, core: 2. Of those that a mesh axis runs over, the one named last changes fastest.
Arguments:
- feature_a: bfloat16 [16, 128, 1024], P('src', 'tgt'), may hold values from -6 to 6
- feature_b: bfloat16 [32, 32, 1024], P('tgt', 'src'), may hold values from -6 to 6
- conv_in: float32 [8, 81], replicated, may hold values from -0.625 to 0.625
- bias_in: float32 [8], replicated, may hold values from -4 to 4
- conv_out: float32 [8, 81], replicated, may hold values from -0.25 to 0.25
Outputs:
- consensus: float32 [32, 32, 16, 128], P('tgt', 'src')
The draws below stay inside these ranges and needn't reach their ends.
All inputs are finite; a program needn't handle non-finite values.
Results may differ from the reference program's by a relative error of at most 0.0024.
Values may be sent and summed in bfloat16 or wider, within the bound.
No kernel may reach another device: no remote copies, remote signals or barrier semaphores. Data moves between devices by JAX's collectives and lax.ppermute only.
A program may use at most 64 MiB of HBM per device.

```python
import jax
import jax.numpy as jnp
from jax import lax

C = 1024
CH = 8
WA = 128
HA = 16
HB = 32
WB = 32


def level_of(stream_key, dims, shards, low, high):
    def one(position, parts):
        steps = jax.random.uniform(jax.random.fold_in(jax.random.fold_in(stream_key, 6), position), (parts,), jnp.float32, low / len(shards), high / len(shards))
        return jnp.repeat(jnp.exp(steps), dims[position] // parts).reshape((-1,) + (1,) * (len(dims) - position - 1))

    loudness = one(*shards[0])
    for cut in shards[1:]:
        loudness = loudness * one(*cut)
    return loudness


def normal_values(stream_key, shape, scale, reach, split=(), kind=jnp.bfloat16):
    result = jax.random.normal(stream_key, shape, jnp.float32) * scale
    if len(split) > 0:
        result = level_of(stream_key, shape, split, -0.22, 0.18) * result
    return jnp.clip(result, min=-reach, max=reach).astype(kind)


def setup_inputs(seed: int = 0) -> dict:
    key_list = jax.random.split(jax.random.key(seed), 6)
    return {
        "feature_a": normal_values(key_list[0], (HA, WA, C), 1.0, 6.0, ((0, 16), (1, 16))),
        "feature_b": normal_values(key_list[1], (HB, WB, C), 1.0, 6.0, ((0, 16), (1, 16))),
        "conv_in": normal_values(key_list[2], (CH, 81), 81 ** -0.5, 0.625, (), jnp.float32),
        "bias_in": normal_values(key_list[3], (CH,), 1.0, 4.0, (), jnp.float32),
        "conv_out": normal_values(key_list[4], (CH, 81), (81 * CH) ** -0.5, 0.25, (), jnp.float32),
    }


def filter_taps(source, weights, extent):
    summed_total = jnp.zeros(extent, jnp.float32)
    for first in range(3):
        for second in range(3):
            for third in range(3):
                for fourth in range(3):
                    weight = weights[first * 27 + second * 9 + third * 3 + fourth]
                    summed_total = summed_total + weight * source[first:first + extent[0], second:second + extent[1], third:third + extent[2], fourth:fourth + extent[3]]
    return summed_total


def network(volume, conv_in, bias_in, conv_out):
    extent = volume.shape
    field = jnp.pad(volume, 1)

    def channel_step(channel_slot, summed_total):
        hidden = jax.nn.relu(filter_taps(field, conv_in[channel_slot], extent) + bias_in[channel_slot])
        padded = jnp.pad(hidden, 1)
        return summed_total + filter_taps(padded, conv_out[channel_slot], extent)

    return lax.fori_loop(0, conv_in.shape[0], channel_step, jnp.zeros(extent, jnp.float32))


def reference(feature_a, feature_b, conv_in, bias_in, conv_out):
    scores = jnp.dot(feature_b.reshape(HB * WB, C), feature_a.reshape(HA * WA, C).T, preferred_element_type=jnp.float32)
    volume = (scores * (C ** -0.5)).astype(jnp.bfloat16).astype(jnp.float32).reshape(HB, WB, HA, WA)
    forward = network(volume, conv_in, bias_in, conv_out)
    mirrored = network(volume.transpose(2, 3, 0, 1), conv_in, bias_in, conv_out).transpose(2, 3, 0, 1)
    return forward + mirrored
```

```python
import jax
import jax.numpy as jnp
import numpy as np
from jax import lax
from jax.experimental import pallas as pl
from jax.experimental.pallas import tpu as pltpu
from jax.sharding import PartitionSpec as P

SHIFTS = (-1, 0, 1)


def mirror_matrix():
    out = np.zeros((81, 81), np.float32)
    for p, q, r, s in np.ndindex(3, 3, 3, 3):
        out[27 * r + 9 * s + 3 * p + q, 27 * p + 9 * q + 3 * r + s] = 1
    return out


def spread_in():
    out = np.zeros((81, 2, 4, 256), np.float32)
    for k2, l, p, q, r, s in np.ndindex(2, 4, 3, 3, 3, 3):
        column = (s * 3 + r) * 24 + (l + q) // 2 * 8 + (k2 + p) * 2 + (l + q) % 2
        out[27 * p + 9 * q + 3 * r + s, k2, l, column] = 1
    return out.reshape(81, 2048)


def spread_out():
    out = np.zeros((81, 4, 4, 128), np.float32)
    for k2, l2, p, q, r, s in np.ndindex(2, 2, 3, 3, 3, 3):
        out[27 * p + 9 * q + 3 * r + s, k2 + p, l2 + q, (r * 3 + s) * 4 + k2 * 2 + l2] = 1
    return out.reshape(81, 2048)


def shifted(x, s):
    if s == 0:
        return x
    lane = lax.broadcasted_iota(jnp.int32, x.shape, 1)
    rolled = pltpu.roll(x, (-s) % 128, 1)
    return jnp.where(lane == (127 if s == 1 else 0), 0.0, rolled)


def weights_kernel(cin_ref, cout_ref, mirror_ref, sel1_ref, sel2_ref, w1_ref, w2_ref):
    def parts(x):
        high = x.astype(jnp.bfloat16)
        low = (x - high.astype(jnp.float32)).astype(jnp.bfloat16)
        rows = []
        for part in (high, low):
            rows.append(part.astype(jnp.float32))
            rows.append(jnp.dot(part, mirror_ref[...], preferred_element_type=jnp.float32))
        return jnp.concatenate(rows, axis=0).astype(jnp.bfloat16)

    t1 = jnp.dot(parts(cin_ref[...]), sel1_ref[...], preferred_element_type=jnp.float32)
    for hl in range(2):
        for kl in range(8):
            row = hl * 128 + kl * 16
            w1_ref[row : row + 16, :] = t1[
                hl * 16 : hl * 16 + 16, kl * 256 : kl * 256 + 256
            ].astype(jnp.bfloat16)
    t2 = jnp.dot(parts(cout_ref[...]), sel2_ref[...], preferred_element_type=jnp.float32)
    rows = []
    for hl in range(2):
        tall = jnp.concatenate(
            [t2[hl * 16 : hl * 16 + 16, kl * 128 : kl * 128 + 128] for kl in range(16)], axis=0
        )
        rows.append(tall.T[:40])
    w2_ref[...] = jnp.concatenate(rows, axis=0).astype(jnp.bfloat16)


def volume_kernel(b_ref, a_ref, o_ref, scr_ref):
    scores = lax.dot_general(
        b_ref[...], a_ref[...], (((1,), (1,)), ((), ())), preferred_element_type=jnp.float32
    ) * (1024 ** -0.5)
    zeros = jnp.zeros((12, 128), jnp.float32)
    scr_ref[0:12, :] = zeros
    scr_ref[204:216, :] = zeros
    for s in range(16):
        scr_ref[12 + 12 * s : 24 + 12 * s, :] = scores[16 * s : 16 * s + 12]
    for s in range(16):
        o_ref[s] = scr_ref[12 * s : 12 * s + 36, :].astype(jnp.bfloat16)


def consensus_kernel(r_ref, w1_ref, w2_ref, bias_ref, o_ref, rf_ref, xs_ref, ps_ref):
    zero_rows = jnp.zeros((24, 256), jnp.float32)
    for n in range(3):
        xs_ref[n, 0] = zero_rows
        xs_ref[n, 17] = zero_rows
    for i in range(16):
        rf_ref[i] = r_ref[i].astype(jnp.float32)
        for half in range(2):
            for ds in range(3):
                rows = rf_ref[i, pl.ds(ds * 12 + half * 4, 8), :]
                for n, s in enumerate(SHIFTS):
                    xs_ref[n, i + 1, ds * 8 : ds * 8 + 8, half * 128 : half * 128 + 128] = shifted(
                        rows, s
                    )
    ps_ref[0:40, :] = jnp.zeros((40, 128), jnp.float32)
    ps_ref[680:720, :] = jnp.zeros((40, 128), jnp.float32)
    pad = jnp.zeros((40, 256), jnp.float32)
    for i in range(0, 16, 2):
        highs, lows = [], []
        for d in range(2):
            rhs = jnp.concatenate(
                [xs_ref[n, i + d + r] for n in range(3) for r in range(3)] + [pad], axis=0
            ).astype(jnp.bfloat16)
            acc = jnp.dot(w1_ref[...], rhs, preferred_element_type=jnp.float32)
            acc = acc[:128] + acc[128:]
            hidden = jnp.concatenate([acc[:, :128], acc[:, 128:]], axis=0)
            hidden = jnp.maximum(hidden + bias_ref[...], 0.0)
            high = hidden.astype(jnp.bfloat16)
            highs.append(high)
            lows.append((hidden - high.astype(jnp.float32)).astype(jnp.bfloat16))
        both = jnp.dot(
            w2_ref[...], jnp.concatenate(highs, axis=1), preferred_element_type=jnp.float32
        )
        more = jnp.dot(
            w2_ref[0:40, :], jnp.concatenate(lows, axis=1), preferred_element_type=jnp.float32
        )
        total = both[:40] + both[40:] + more
        ps_ref[40 * (i + 1) : 40 * (i + 2), :] = total[:, :128]
        ps_ref[40 * (i + 2) : 40 * (i + 3), :] = total[:, 128:]
    for kl in range(4):
        out = None
        for n, s in enumerate(SHIFTS):
            part = None
            for r in range(3):
                rows = ps_ref[pl.ds(40 * r + (r * 3 + n) * 4 + kl, 16, stride=40), :]
                part = rows if part is None else part + rows
            part = shifted(part, s)
            out = part if out is None else out + part
        o_ref[kl * 16 : kl * 16 + 16, :] = out


VMEM = pl.BlockSpec(memory_space=pltpu.VMEM)


def call(kernel, outs, scratch, flops, *args):
    return pl.pallas_call(
        kernel,
        out_shape=outs,
        in_specs=[VMEM] * len(args),
        out_specs=jax.tree.map(lambda _: VMEM, outs),
        scratch_shapes=scratch,
        compiler_params=pltpu.CompilerParams(vmem_limit_bytes=16 << 20),
        cost_estimate=pl.CostEstimate(flops=flops, bytes_accessed=1 << 20, transcendentals=0),
    )(*args)


def per_device(feature_a, feature_b, conv_in, bias_in, conv_out):
    count = lax.axis_size("tgt")
    up = [(i, i + 1) for i in range(count - 1)]
    down = [(i + 1, i) for i in range(count - 1)]
    low = lax.ppermute(feature_b, "tgt", up)
    high = lax.ppermute(feature_b, "tgt", down)
    wide = lax.all_to_all(
        jnp.broadcast_to(feature_a, (16, 8, 1024)), "tgt", 0, 0, tiled=True
    ).reshape(128, 1024)
    tall = jnp.concatenate([low, feature_b, high, jnp.zeros_like(feature_b)], axis=0)
    tall = lax.all_to_all(
        jnp.broadcast_to(tall.reshape(1, 16, 1024), (16, 16, 1024)), "src", 0, 0, tiled=True
    ).reshape(256, 1024)
    w1, w2 = call(
        weights_kernel,
        (
            jax.ShapeDtypeStruct((256, 256), jnp.bfloat16),
            jax.ShapeDtypeStruct((80, 256), jnp.bfloat16),
        ),
        [],
        1 << 24,
        conv_in,
        conv_out,
        jnp.asarray(mirror_matrix(), jnp.bfloat16),
        jnp.asarray(spread_in(), jnp.bfloat16),
        jnp.asarray(spread_out(), jnp.bfloat16),
    )
    row = lax.axis_index("tgt") * 2 - 1 + jnp.arange(4)
    column = lax.axis_index("src") * 2 - 1 + jnp.arange(4)
    inside = ((row >= 0) & (row < 32))[:, None] & ((column >= 0) & (column < 32))[None, :]
    bias = jnp.where(
        inside[:, :, None, None, None], bias_in[None, None, None, :, None], -1e30
    )
    bias = jnp.broadcast_to(bias, (4, 4, 2, 8, 128)).reshape(256, 128)
    pieces = call(
        volume_kernel,
        jax.ShapeDtypeStruct((16, 36, 128), jnp.bfloat16),
        [pltpu.VMEM((216, 128), jnp.float32)],
        1 << 26,
        tall,
        wide,
    )
    pieces = lax.all_to_all(pieces, "src", 0, 0, tiled=True)
    out = call(
        consensus_kernel,
        jax.ShapeDtypeStruct((64, 128), jnp.float32),
        [
            pltpu.VMEM((16, 36, 128), jnp.float32),
            pltpu.VMEM((3, 18, 24, 256), jnp.float32),
            pltpu.VMEM((720, 128), jnp.float32),
        ],
        1 << 28,
        pieces,
        w1,
        w2,
        bias,
    )
    return out.reshape(2, 2, 16, 128)


def solution(mesh):
    in_specs = (P("src", "tgt", None), P("tgt", "src", None), P(), P(), P())
    out_specs = P("tgt", "src", None, None)
    return jax.shard_map(
        per_device, mesh=mesh, in_specs=in_specs, out_specs=out_specs, check_vma=False
    )
```

```python
import jax
import jax.numpy as jnp
import numpy as np
from jax import lax
from jax.experimental import pallas as pl
from jax.experimental.pallas import tpu as pltpu
from jax.sharding import PartitionSpec as P

SHIFTS = (-1, 0, 1)


def mirror_matrix():
    out = np.zeros((81, 81), np.float32)
    for p, q, r, s in np.ndindex(3, 3, 3, 3):
        out[27 * r + 9 * s + 3 * p + q, 27 * p + 9 * q + 3 * r + s] = 1
    return out


def spread_in():
    out = np.zeros((81, 2, 4, 256), np.float32)
    for k2, l, p, q, r, s in np.ndindex(2, 4, 3, 3, 3, 3):
        k, c = k2 + p, l + q
        column = (s * 3 + r) * 24 + k // 2 * 12 + c // 2 * 4 + k % 2 * 2 + c % 2
        out[27 * p + 9 * q + 3 * r + s, k2, l, column] = 1
    return out.reshape(81, 2048)


def spread_out():
    out = np.zeros((81, 4, 4, 128), np.float32)
    for k2, l2, p, q, r, s in np.ndindex(2, 2, 3, 3, 3, 3):
        out[27 * p + 9 * q + 3 * r + s, k2 + p, l2 + q, (r * 3 + s) * 4 + k2 * 2 + l2] = 1
    return out.reshape(81, 2048)


def shifted(x, s):
    if s == 0:
        return x
    lane = lax.broadcasted_iota(jnp.int32, x.shape, 1)
    rolled = pltpu.roll(x, (-s) % 128, 1)
    return jnp.where(lane == (127 if s == 1 else 0), 0.0, rolled)


def weights_kernel(cin_ref, cout_ref, mirror_ref, sel1_ref, sel2_ref, w1_ref, w2_ref):
    def parts(x):
        high = x.astype(jnp.bfloat16)
        low = (x - high.astype(jnp.float32)).astype(jnp.bfloat16)
        rows = []
        for part in (high, low):
            rows.append(part.astype(jnp.float32))
            rows.append(jnp.dot(part, mirror_ref[...], preferred_element_type=jnp.float32))
        return jnp.concatenate(rows, axis=0).astype(jnp.bfloat16)

    t1 = jnp.dot(parts(cin_ref[...]), sel1_ref[...], preferred_element_type=jnp.float32)
    for hl in range(2):
        for kl in range(8):
            row = hl * 128 + kl * 16
            w1_ref[row : row + 16, :] = t1[
                hl * 16 : hl * 16 + 16, kl * 256 : kl * 256 + 256
            ].astype(jnp.bfloat16)
    t2 = jnp.dot(parts(cout_ref[...]), sel2_ref[...], preferred_element_type=jnp.float32)
    rows = []
    for hl in range(2):
        tall = jnp.concatenate(
            [t2[hl * 16 : hl * 16 + 16, kl * 128 : kl * 128 + 128] for kl in range(16)], axis=0
        )
        rows.append(tall.T[:40])
    w2_ref[...] = jnp.concatenate(rows, axis=0).astype(jnp.bfloat16)


def volume_kernel(low_ref, own_ref, high_ref, a_ref, o_ref, scr_ref, tmp_ref):
    tall = jnp.concatenate([low_ref[...], own_ref[...], high_ref[...]], axis=0)
    scores = lax.dot_general(
        tall, a_ref[...], (((1,), (1,)), ((), ())), preferred_element_type=jnp.float32
    ) * (1024 ** -0.5)
    zeros = jnp.zeros((8, 128), jnp.float32)
    for n in range(3):
        scr_ref[n, 0:8, :] = zeros
        scr_ref[n, 8:72, :] = scores[64 * n : 64 * n + 64]
        scr_ref[n, 72:80, :] = zeros
    for s in range(16):
        for n in range(3):
            tmp_ref[s, 12 * n : 12 * n + 12, :] = scr_ref[n, 4 + 4 * s : 16 + 4 * s, :]
        o_ref[s] = tmp_ref[s, 0:36, :].astype(jnp.bfloat16)


def consensus_kernel(r_ref, w1_ref, w2_ref, bias_ref, o_ref, rf_ref, xs_ref, ps_ref):
    zero_rows = jnp.zeros((24, 256), jnp.float32)
    for n in range(3):
        xs_ref[n, 0] = zero_rows
        xs_ref[n, 17] = zero_rows
    for i in range(16):
        rf_ref[i] = r_ref[i].astype(jnp.float32)
        for half in range(2):
            for d in range(0, 24, 8):
                rows = rf_ref[i, pl.ds(half * 12 + d, 8), :]
                for n, s in enumerate(SHIFTS):
                    xs_ref[n, i + 1, d : d + 8, half * 128 : half * 128 + 128] = shifted(rows, s)
    ps_ref[0:40, :] = jnp.zeros((40, 128), jnp.float32)
    ps_ref[680:720, :] = jnp.zeros((40, 128), jnp.float32)
    pad = jnp.zeros((40, 256), jnp.float32)
    for i in range(0, 16, 2):
        highs, lows = [], []
        for d in range(2):
            rhs = jnp.concatenate(
                [xs_ref[n, i + d + r] for n in range(3) for r in range(3)] + [pad], axis=0
            ).astype(jnp.bfloat16)
            acc = jnp.dot(w1_ref[...], rhs, preferred_element_type=jnp.float32)
            acc = acc[:128] + acc[128:]
            hidden = jnp.concatenate([acc[:, :128], acc[:, 128:]], axis=0)
            hidden = jnp.maximum(hidden + bias_ref[...], 0.0)
            high = hidden.astype(jnp.bfloat16)
            highs.append(high)
            lows.append((hidden - high.astype(jnp.float32)).astype(jnp.bfloat16))
        both = jnp.dot(
            w2_ref[...], jnp.concatenate(highs, axis=1), preferred_element_type=jnp.float32
        )
        more = jnp.dot(
            w2_ref[0:40, :], jnp.concatenate(lows, axis=1), preferred_element_type=jnp.float32
        )
        total = both[:40] + both[40:] + more
        ps_ref[40 * (i + 1) : 40 * (i + 2), :] = total[:, :128]
        ps_ref[40 * (i + 2) : 40 * (i + 3), :] = total[:, 128:]
    for kl in range(4):
        out = None
        for n, s in enumerate(SHIFTS):
            part = None
            for r in range(3):
                rows = ps_ref[pl.ds(40 * r + (r * 3 + n) * 4 + kl, 16, stride=40), :]
                part = rows if part is None else part + rows
            part = shifted(part, s)
            out = part if out is None else out + part
        o_ref[kl * 16 : kl * 16 + 16, :] = out


VMEM = pl.BlockSpec(memory_space=pltpu.VMEM)


def call(kernel, outs, scratch, flops, *args):
    return pl.pallas_call(
        kernel,
        out_shape=outs,
        in_specs=[VMEM] * len(args),
        out_specs=jax.tree.map(lambda _: VMEM, outs),
        scratch_shapes=scratch,
        compiler_params=pltpu.CompilerParams(vmem_limit_bytes=16 << 20),
        cost_estimate=pl.CostEstimate(flops=flops, bytes_accessed=1 << 20, transcendentals=0),
    )(*args)


def per_device(feature_a, feature_b, conv_in, bias_in, conv_out):
    b = lax.all_to_all(
        jnp.broadcast_to(feature_b.reshape(1, 4, 1024), (16, 4, 1024)), "src", 0, 0, tiled=True
    ).reshape(64, 1024)
    other = lax.ppermute(feature_a, "yh", [(0, 1), (1, 0)])
    first = lax.axis_index("yh") == 0
    wide = jnp.concatenate(
        [jnp.where(first, feature_a, other), jnp.where(first, other, feature_a)], axis=1
    )
    wide = lax.all_to_all(
        jnp.broadcast_to(wide, (8, 16, 1024)), "z", 0, 0, tiled=True
    ).reshape(128, 1024)
    up = [(i, i + 1) for i in range(15)]
    down = [(i + 1, i) for i in range(15)]
    low = lax.ppermute(b, ("z", "yh"), up)
    high = lax.ppermute(b, ("z", "yh"), down)
    w1, w2 = call(
        weights_kernel,
        (
            jax.ShapeDtypeStruct((256, 256), jnp.bfloat16),
            jax.ShapeDtypeStruct((80, 256), jnp.bfloat16),
        ),
        [],
        1 << 24,
        conv_in,
        conv_out,
        jnp.asarray(mirror_matrix(), jnp.bfloat16),
        jnp.asarray(spread_in(), jnp.bfloat16),
        jnp.asarray(spread_out(), jnp.bfloat16),
    )
    row = lax.axis_index(("z", "yh")) * 2 - 1 + jnp.arange(4)
    column = lax.axis_index("src") * 2 - 1 + jnp.arange(4)
    inside = ((row >= 0) & (row < 32))[:, None] & ((column >= 0) & (column < 32))[None, :]
    bias = jnp.where(
        inside[:, :, None, None, None], bias_in[None, None, None, :, None], -1e30
    )
    bias = jnp.broadcast_to(bias, (4, 4, 2, 8, 128)).reshape(256, 128)
    pieces = call(
        volume_kernel,
        jax.ShapeDtypeStruct((16, 36, 128), jnp.bfloat16),
        [pltpu.VMEM((3, 80, 128), jnp.float32), pltpu.VMEM((16, 40, 128), jnp.float32)],
        1 << 26,
        low,
        b,
        high,
        wide,
    )
    pieces = lax.all_to_all(pieces, "src", 0, 0, tiled=True)
    out = call(
        consensus_kernel,
        jax.ShapeDtypeStruct((64, 128), jnp.float32),
        [
            pltpu.VMEM((16, 36, 128), jnp.float32),
            pltpu.VMEM((3, 18, 24, 256), jnp.float32),
            pltpu.VMEM((720, 128), jnp.float32),
        ],
        1 << 28,
        pieces,
        w1,
        w2,
        bias,
    )
    return out.reshape(2, 2, 16, 128)


def solution(mesh):
    mesh = jax.sharding.Mesh(mesh.devices.reshape(16, 8, 2), ("src", "z", "yh"))
    tgt = ("z", "yh")
    in_specs = (P("src", tgt, None), P(tgt, "src", None), P(), P(), P())
    out_specs = P(tgt, "src", None, None)
    return jax.shard_map(
        per_device, mesh=mesh, in_specs=in_specs, out_specs=out_specs, check_vma=False
    )
```

```python
import jax
import jax.numpy as jnp
import numpy as np
from jax import lax
from jax.experimental import pallas as pl
from jax.experimental.pallas import tpu as pltpu
from jax.sharding import PartitionSpec as P


SHIFTS = (-1, 0, 1)


def mirror_matrix():
    out = np.zeros((81, 81), np.float32)
    for p, q, r, s in np.ndindex(3, 3, 3, 3):
        out[27 * r + 9 * s + 3 * p + q, 27 * p + 9 * q + 3 * r + s] = 1
    return out


def spread_in():
    out = np.zeros((81, 2, 4, 256), np.float32)
    for k2, l, p, q, r, s in np.ndindex(2, 4, 3, 3, 3, 3):
        k, c = k2 + p, l + q
        column = (s * 3 + r) * 24 + k // 2 * 12 + c // 2 * 4 + k % 2 * 2 + c % 2
        out[27 * p + 9 * q + 3 * r + s, k2, l, column] = 1
    return out.reshape(81, 2048)


def spread_out():
    out = np.zeros((81, 4, 4, 128), np.float32)
    for k2, l2, p, q, r, s in np.ndindex(2, 2, 3, 3, 3, 3):
        out[27 * p + 9 * q + 3 * r + s, k2 + p, l2 + q, (r * 3 + s) * 4 + k2 * 2 + l2] = 1
    return out.reshape(81, 2048)


def shifted(x, s):
    if s == 0:
        return x
    lane = lax.broadcasted_iota(jnp.int32, x.shape, 1)
    rolled = pltpu.roll(x, (-s) % 128, 1)
    return jnp.where(lane == (127 if s == 1 else 0), 0.0, rolled)


def weights_kernel(cin_ref, cout_ref, mirror_ref, sel1_ref, sel2_ref, w1_ref, w2_ref):
    def parts(x):
        high = x.astype(jnp.bfloat16)
        low = (x - high.astype(jnp.float32)).astype(jnp.bfloat16)
        rows = []
        for part in (high, low):
            rows.append(part.astype(jnp.float32))
            rows.append(jnp.dot(part, mirror_ref[...], preferred_element_type=jnp.float32))
        return jnp.concatenate(rows, axis=0).astype(jnp.bfloat16)

    t1 = jnp.dot(parts(cin_ref[...]), sel1_ref[...], preferred_element_type=jnp.float32)
    for hl in range(2):
        for kl in range(8):
            row = hl * 128 + kl * 16
            w1_ref[row : row + 16, :] = t1[
                hl * 16 : hl * 16 + 16, kl * 256 : kl * 256 + 256
            ].astype(jnp.bfloat16)
    t2 = jnp.dot(parts(cout_ref[...]), sel2_ref[...], preferred_element_type=jnp.float32)
    rows = []
    for hl in range(2):
        tall = jnp.concatenate(
            [t2[hl * 16 : hl * 16 + 16, kl * 128 : kl * 128 + 128] for kl in range(16)], axis=0
        )
        rows.append(tall.T[:40])
    w2_ref[...] = jnp.concatenate(rows, axis=0).astype(jnp.bfloat16)


def store_copies(source, target, sems):
    stores = [
        pltpu.make_async_copy(source, target.at[n], sems.at[n]) for n in range(target.shape[0])
    ]
    for store in stores:
        store.start()
    for store in stores:
        store.wait()


def b_copies_kernel(b_ref, o_ref, out_sem):
    store_copies(b_ref, o_ref, out_sem)


def a_copies_kernel(mine_ref, other_ref, y_ref, o_ref, v_ref, out_sem):
    first = y_ref[0] == 0
    mine, other = mine_ref[...], other_ref[...]
    v_ref[0] = jnp.where(first, mine, other)
    v_ref[1] = jnp.where(first, other, mine)
    store_copies(v_ref, o_ref, out_sem)


def volume_kernel(far_ref, own_ref, near_ref, a_ref, y_ref, o_ref, scr_ref, tmp_ref):
    tall = jnp.concatenate([far_ref[...], own_ref[...], near_ref[...]], axis=0)
    scores = lax.dot_general(
        tall, a_ref[...], (((1,), (1,)), ((), ())), preferred_element_type=jnp.float32
    ) * (1024 ** -0.5)
    zeros = jnp.zeros((8, 128), jnp.float32)
    far = 2 * y_ref[0]
    for n, slot in enumerate((far, 1, 2 - far)):
        scr_ref[slot, 0:8, :] = zeros
        scr_ref[slot, 8:72, :] = scores[64 * n : 64 * n + 64]
        scr_ref[slot, 72:80, :] = zeros
    for s in range(16):
        for n in range(3):
            tmp_ref[s, 12 * n : 12 * n + 12, :] = scr_ref[n, 4 + 4 * s : 16 + 4 * s, :]
        o_ref[s] = tmp_ref[s, 0:36, :].astype(jnp.bfloat16)


def consensus_kernel(r_ref, w1_ref, w2_ref, bias_ref, o_ref, rf_ref, xs_ref, ps_ref):
    zero_rows = jnp.zeros((24, 256), jnp.float32)
    for n in range(3):
        xs_ref[n, 0] = zero_rows
        xs_ref[n, 17] = zero_rows
    for i in range(16):
        rf_ref[i] = r_ref[i].astype(jnp.float32)
        for half in range(2):
            for d in range(0, 24, 8):
                rows = rf_ref[i, pl.ds(half * 12 + d, 8), :]
                for n, s in enumerate(SHIFTS):
                    xs_ref[n, i + 1, d : d + 8, half * 128 : half * 128 + 128] = shifted(rows, s)
    ps_ref[0:40, :] = jnp.zeros((40, 128), jnp.float32)
    ps_ref[680:720, :] = jnp.zeros((40, 128), jnp.float32)
    pad = jnp.zeros((40, 256), jnp.float32)
    for i in range(0, 16, 2):
        highs, lows = [], []
        for d in range(2):
            rhs = jnp.concatenate(
                [xs_ref[n, i + d + r] for n in range(3) for r in range(3)] + [pad], axis=0
            ).astype(jnp.bfloat16)
            acc = jnp.dot(w1_ref[...], rhs, preferred_element_type=jnp.float32)
            acc = acc[:128] + acc[128:]
            hidden = jnp.concatenate([acc[:, :128], acc[:, 128:]], axis=0)
            hidden = jnp.maximum(hidden + bias_ref[...], 0.0)
            high = hidden.astype(jnp.bfloat16)
            highs.append(high)
            lows.append((hidden - high.astype(jnp.float32)).astype(jnp.bfloat16))
        both = jnp.dot(
            w2_ref[...], jnp.concatenate(highs, axis=1), preferred_element_type=jnp.float32
        )
        more = jnp.dot(
            w2_ref[0:40, :], jnp.concatenate(lows, axis=1), preferred_element_type=jnp.float32
        )
        total = both[:40] + both[40:] + more
        ps_ref[40 * (i + 1) : 40 * (i + 2), :] = total[:, :128]
        ps_ref[40 * (i + 2) : 40 * (i + 3), :] = total[:, 128:]
    for kl in range(4):
        out = None
        for n, s in enumerate(SHIFTS):
            part = None
            for r in range(3):
                rows = ps_ref[pl.ds(40 * r + (r * 3 + n) * 4 + kl, 16, stride=40), :]
                part = rows if part is None else part + rows
            part = shifted(part, s)
            out = part if out is None else out + part
        o_ref[kl * 16 : kl * 16 + 16, :] = out


VMEM = pl.BlockSpec(memory_space=pltpu.VMEM)
SMEM = pl.BlockSpec(memory_space=pltpu.SMEM)
HBM = pl.BlockSpec(memory_space=pltpu.HBM)


def call(kernel, outs, scratch, flops, *args):
    return pl.pallas_call(
        kernel,
        out_shape=outs,
        in_specs=[VMEM] * len(args),
        out_specs=jax.tree.map(lambda _: VMEM, outs),
        scratch_shapes=scratch,
        compiler_params=pltpu.CompilerParams(vmem_limit_bytes=16 << 20),
        cost_estimate=pl.CostEstimate(flops=flops, bytes_accessed=1 << 20, transcendentals=0),
    )(*args)


def per_device(feature_a, feature_b, conv_in, bias_in, conv_out):
    y_half = lax.axis_index("yh").reshape(1)
    b = pl.pallas_call(
        b_copies_kernel,
        out_shape=jax.ShapeDtypeStruct((16, 2, 2, 1024), jnp.bfloat16),
        in_specs=[VMEM],
        out_specs=HBM,
        scratch_shapes=[pltpu.SemaphoreType.DMA((16,))],
        compiler_params=pltpu.CompilerParams(vmem_limit_bytes=16 << 20),
    )(feature_b)
    b = lax.all_to_all(b, "src", 0, 0, tiled=True)
    b = b.reshape(64, 1024)
    other = lax.ppermute(feature_a, "yh", [(0, 1), (1, 0)])
    wide = pl.pallas_call(
        a_copies_kernel,
        out_shape=jax.ShapeDtypeStruct((8, 2, 8, 1024), jnp.bfloat16),
        in_specs=[VMEM, VMEM, SMEM],
        out_specs=HBM,
        scratch_shapes=[
            pltpu.VMEM((2, 8, 1024), jnp.bfloat16),
            pltpu.SemaphoreType.DMA((8,)),
        ],
        compiler_params=pltpu.CompilerParams(vmem_limit_bytes=16 << 20),
    )(feature_a[0], other[0], y_half)
    wide = lax.all_to_all(wide, "z", 0, 0, tiled=True)
    wide = wide.reshape(128, 1024)
    near = [(2 * z + y, 2 * z + 1 - y) for z in range(8) for y in range(2)]
    far = [(2 * z + 1, 2 * z + 2) for z in range(7)]
    far += [(target, source) for source, target in far]
    near = lax.ppermute(b, ("z", "yh"), near)
    far = lax.ppermute(b, ("z", "yh"), far)
    w1, w2 = call(
        weights_kernel,
        (
            jax.ShapeDtypeStruct((256, 256), jnp.bfloat16),
            jax.ShapeDtypeStruct((80, 256), jnp.bfloat16),
        ),
        [],
        1 << 24,
        conv_in,
        conv_out,
        jnp.asarray(mirror_matrix(), jnp.bfloat16),
        jnp.asarray(spread_in(), jnp.bfloat16),
        jnp.asarray(spread_out(), jnp.bfloat16),
    )
    row = lax.axis_index(("z", "yh")) * 2 - 1 + jnp.arange(4)
    column = lax.axis_index("src") * 2 - 1 + jnp.arange(4)
    inside = ((row >= 0) & (row < 32))[:, None] & ((column >= 0) & (column < 32))[None, :]
    bias = jnp.where(
        inside[:, :, None, None, None], bias_in[None, None, None, :, None], -1e30
    )
    bias = jnp.broadcast_to(bias, (4, 4, 2, 8, 128)).reshape(256, 128)
    pieces = pl.pallas_call(
        volume_kernel,
        out_shape=jax.ShapeDtypeStruct((16, 36, 128), jnp.bfloat16),
        in_specs=[VMEM] * 4 + [SMEM],
        out_specs=VMEM,
        scratch_shapes=[
            pltpu.VMEM((3, 80, 128), jnp.float32),
            pltpu.VMEM((16, 40, 128), jnp.float32),
        ],
        compiler_params=pltpu.CompilerParams(vmem_limit_bytes=16 << 20),
        cost_estimate=pl.CostEstimate(flops=1 << 26, bytes_accessed=1 << 20, transcendentals=0),
    )(far, b, near, wide, y_half)
    pieces = lax.all_to_all(pieces, "src", 0, 0, tiled=True)
    out = call(
        consensus_kernel,
        jax.ShapeDtypeStruct((64, 128), jnp.float32),
        [
            pltpu.VMEM((16, 36, 128), jnp.float32),
            pltpu.VMEM((3, 18, 24, 256), jnp.float32),
            pltpu.VMEM((720, 128), jnp.float32),
        ],
        1 << 28,
        pieces,
        w1,
        w2,
        bias,
    )
    return out.reshape(2, 2, 16, 128)


def solution(mesh):
    mesh = jax.sharding.Mesh(mesh.devices.reshape(16, 8, 2), ("src", "z", "yh"))
    tgt = ("z", "yh")
    in_specs = (P("src", tgt, None), P(tgt, "src", None), P(), P(), P())
    out_specs = P(tgt, "src", None, None)
    return jax.shard_map(
        per_device, mesh=mesh, in_specs=in_specs, out_specs=out_specs, check_vma=False
    )
```

```python
import jax
import jax.numpy as jnp
import numpy as np
from jax import lax
from jax.experimental import pallas as pl
from jax.experimental.pallas import tpu as pltpu
from jax.sharding import PartitionSpec as P


SHIFTS = (-1, 0, 1)


def mirror_matrix():
    out = np.zeros((81, 81), np.float32)
    for p, q, r, s in np.ndindex(3, 3, 3, 3):
        out[27 * r + 9 * s + 3 * p + q, 27 * p + 9 * q + 3 * r + s] = 1
    return out


def spread_in():
    out = np.zeros((81, 2, 4, 256), np.float32)
    for k2, l, p, q, r, s in np.ndindex(2, 4, 3, 3, 3, 3):
        k, c = k2 + p, l + q
        column = r * 80 + s * 24 + k // 2 * 12 + c // 2 * 4 + k % 2 * 2 + c % 2
        out[27 * p + 9 * q + 3 * r + s, k2, l, column] = 1
    return out.reshape(81, 2048)


def spread_out():
    out = np.zeros((81, 4, 4, 128), np.float32)
    for k2, l2, p, q, r, s in np.ndindex(2, 2, 3, 3, 3, 3):
        out[27 * p + 9 * q + 3 * r + s, k2 + p, l2 + q, (r * 3 + s) * 4 + k2 * 2 + l2] = 1
    return out.reshape(81, 2048)


def shifted(x, s):
    if s == 0:
        return x
    lane = lax.broadcasted_iota(jnp.int32, x.shape, 1)
    rolled = pltpu.roll(x, (-s) % 128, 1)
    return jnp.where(lane == (127 if s == 1 else 0), 0.0, rolled)


def weights_kernel(
    cin_ref, cout_ref, mirror_ref, sel1_ref, sel2_ref, bias_ref, at_ref, w1_ref, w2_ref
):
    def parts(x):
        high = x.astype(jnp.bfloat16)
        low = (x - high.astype(jnp.float32)).astype(jnp.bfloat16)
        rows = []
        for part in (high, low):
            rows.append(part.astype(jnp.float32))
            rows.append(jnp.dot(part, mirror_ref[...], preferred_element_type=jnp.float32))
        return jnp.concatenate(rows, axis=0).astype(jnp.bfloat16)

    t1 = jnp.dot(parts(cin_ref[...]), sel1_ref[...], preferred_element_type=jnp.float32)
    lane = lax.broadcasted_iota(jnp.int32, (16, 256), 1)
    bias = bias_ref[...]
    high = bias.astype(jnp.bfloat16).astype(jnp.float32)
    for hl, part in enumerate((high, bias - high)):
        for kl in range(8):
            block = t1[hl * 16 : hl * 16 + 16, kl * 256 : kl * 256 + 256]
            for half in range(2):
                row, column = at_ref[0] + half * 2 + kl // 4, at_ref[1] + kl % 4
                inside = (row >= 0) & (row < 32) & (column >= 0) & (column < 32)
                block = jnp.where(
                    lane == 152 + half, jnp.where(inside, part, -1e30 if hl == 0 else 0.0), block
                )
            row = hl * 128 + kl * 16
            w1_ref[row : row + 16, :] = block.astype(jnp.bfloat16)
    t2 = jnp.dot(parts(cout_ref[...]), sel2_ref[...], preferred_element_type=jnp.float32)
    rows = []
    for hl in range(2):
        tall = jnp.concatenate(
            [t2[hl * 16 : hl * 16 + 16, kl * 128 : kl * 128 + 128] for kl in range(16)], axis=0
        )
        rows.append(tall.T[:40])
    w2_ref[...] = jnp.concatenate(rows, axis=0).astype(jnp.bfloat16)


def store_copies(source, target, sems):
    stores = [
        pltpu.make_async_copy(source, target.at[n], sems.at[n]) for n in range(target.shape[0])
    ]
    for store in stores:
        store.start()
    for store in stores:
        store.wait()


def b_copies_kernel(b_ref, o_ref, out_sem):
    store_copies(b_ref, o_ref, out_sem)


def a_copies_kernel(mine_ref, other_ref, y_ref, o_ref, v_ref, out_sem):
    first = y_ref[0] == 0
    mine, other = mine_ref[...], other_ref[...]
    v_ref[0] = jnp.where(first, mine, other)
    v_ref[1] = jnp.where(first, other, mine)
    store_copies(v_ref, o_ref, out_sem)


def volume_kernel(far_ref, own_ref, near_ref, a_ref, y_ref, o_ref, scr_ref, tmp_ref):
    tall = jnp.concatenate([far_ref[...], own_ref[...], near_ref[...]], axis=0)
    scores = lax.dot_general(
        tall, a_ref[...], (((1,), (1,)), ((), ())), preferred_element_type=jnp.float32
    ) * (1024 ** -0.5)
    zeros = jnp.zeros((8, 128), jnp.float32)
    far = 2 * y_ref[0]
    for n, slot in enumerate((far, 1, 2 - far)):
        scr_ref[slot, 0:8, :] = zeros
        scr_ref[slot, 8:72, :] = scores[64 * n : 64 * n + 64]
        scr_ref[slot, 72:80, :] = zeros
    for s in range(16):
        for n in range(3):
            tmp_ref[s, 12 * n : 12 * n + 12, :] = scr_ref[n, 4 + 4 * s : 16 + 4 * s, :]
        o_ref[s] = tmp_ref[s, 0:36, :].astype(jnp.bfloat16)


def consensus_kernel(r_ref, w1_ref, w2_ref, o_ref, rf_ref, xs_ref, ps_ref):
    xs_ref[0:80, :] = jnp.zeros((80, 256), jnp.bfloat16)
    xs_ref[1360:1456, :] = jnp.zeros((96, 256), jnp.bfloat16)
    sublane = lax.broadcasted_iota(jnp.int32, (8, 128), 0)
    for i in range(16):
        rf_ref[i] = r_ref[i].astype(jnp.float32)
        for half in range(2):
            rows = [rf_ref[i, pl.ds(half * 12 + d, 8), :] for d in range(0, 24, 8)]
            rows = [shifted(x, s) for s in SHIFTS for x in rows]
            rows.append(jnp.where(sublane == half, 1.0, 0.0))
            xs_ref[80 * (i + 1) : 80 * (i + 2), half * 128 : half * 128 + 128] = jnp.concatenate(
                rows, axis=0
            ).astype(jnp.bfloat16)
    ps_ref[0:40, :] = jnp.zeros((40, 128), jnp.float32)
    ps_ref[680:720, :] = jnp.zeros((40, 128), jnp.float32)

    def second(i, highs, lows):
        both = jnp.dot(
            w2_ref[...], jnp.concatenate(highs, axis=1), preferred_element_type=jnp.float32
        )
        more = jnp.dot(
            w2_ref[0:40, :], jnp.concatenate(lows, axis=1), preferred_element_type=jnp.float32
        )
        total = both[:40] + both[40:] + more
        ps_ref[40 * (i + 1) : 40 * (i + 2), :] = total[:, :128]
        ps_ref[40 * (i + 2) : 40 * (i + 3), :] = total[:, 128:]

    def first(i):
        rhs = xs_ref[80 * i : 80 * i + 256, :]
        return jnp.dot(w1_ref[...], rhs, preferred_element_type=jnp.float32)

    def split(acc):
        acc = acc[:128] + acc[128:]
        hidden = jnp.maximum(jnp.concatenate([acc[:, :128], acc[:, 128:]], axis=0), 0.0)
        high = hidden.astype(jnp.bfloat16)
        return high, (hidden - high.astype(jnp.float32)).astype(jnp.bfloat16)

    done = None
    for i in range(0, 16, 2):
        sums = [first(i), first(i + 1)]
        if done is not None:
            second(i - 2, *done)
        done = tuple(zip(*[split(x) for x in sums]))
    second(14, *done)
    for kl in range(4):
        out = None
        for n, s in enumerate(SHIFTS):
            part = None
            for r in range(3):
                rows = ps_ref[pl.ds(40 * r + (r * 3 + n) * 4 + kl, 16, stride=40), :]
                part = rows if part is None else part + rows
            part = shifted(part, s)
            out = part if out is None else out + part
        o_ref[kl * 16 : kl * 16 + 16, :] = out


VMEM = pl.BlockSpec(memory_space=pltpu.VMEM)
SMEM = pl.BlockSpec(memory_space=pltpu.SMEM)
HBM = pl.BlockSpec(memory_space=pltpu.HBM)


def call(kernel, outs, scratch, flops, *args):
    return pl.pallas_call(
        kernel,
        out_shape=outs,
        in_specs=[VMEM] * len(args),
        out_specs=jax.tree.map(lambda _: VMEM, outs),
        scratch_shapes=scratch,
        compiler_params=pltpu.CompilerParams(vmem_limit_bytes=16 << 20),
        cost_estimate=pl.CostEstimate(flops=flops, bytes_accessed=1 << 20, transcendentals=0),
    )(*args)


def per_device(feature_a, feature_b, conv_in, bias_in, conv_out):
    y_half = lax.axis_index("yh").reshape(1)
    b = pl.pallas_call(
        b_copies_kernel,
        out_shape=jax.ShapeDtypeStruct((16, 2, 2, 1024), jnp.bfloat16),
        in_specs=[VMEM],
        out_specs=HBM,
        scratch_shapes=[pltpu.SemaphoreType.DMA((16,))],
        compiler_params=pltpu.CompilerParams(vmem_limit_bytes=16 << 20),
    )(feature_b)
    b = lax.all_to_all(b, "src", 0, 0, tiled=True)
    b = b.reshape(64, 1024)
    other = lax.ppermute(feature_a, "yh", [(0, 1), (1, 0)])
    wide = pl.pallas_call(
        a_copies_kernel,
        out_shape=jax.ShapeDtypeStruct((8, 2, 8, 1024), jnp.bfloat16),
        in_specs=[VMEM, VMEM, SMEM],
        out_specs=HBM,
        scratch_shapes=[
            pltpu.VMEM((2, 8, 1024), jnp.bfloat16),
            pltpu.SemaphoreType.DMA((8,)),
        ],
        compiler_params=pltpu.CompilerParams(vmem_limit_bytes=16 << 20),
    )(feature_a[0], other[0], y_half)
    wide = lax.all_to_all(wide, "z", 0, 0, tiled=True)
    wide = wide.reshape(128, 1024)
    near = [(2 * z + y, 2 * z + 1 - y) for z in range(8) for y in range(2)]
    far = [(2 * z + 1, 2 * z + 2) for z in range(7)]
    far += [(target, source) for source, target in far]
    near = lax.ppermute(b, ("z", "yh"), near)
    far = lax.ppermute(b, ("z", "yh"), far)
    at = jnp.stack([lax.axis_index(("z", "yh")) * 2 - 1, lax.axis_index("src") * 2 - 1])
    w1, w2 = pl.pallas_call(
        weights_kernel,
        out_shape=(
            jax.ShapeDtypeStruct((256, 256), jnp.bfloat16),
            jax.ShapeDtypeStruct((80, 256), jnp.bfloat16),
        ),
        in_specs=[VMEM] * 6 + [SMEM],
        out_specs=(VMEM,) * 2,
        compiler_params=pltpu.CompilerParams(vmem_limit_bytes=16 << 20),
        cost_estimate=pl.CostEstimate(
            flops=1 << 24, bytes_accessed=1 << 20, transcendentals=0
        ),
    )(
        conv_in,
        conv_out,
        jnp.asarray(mirror_matrix(), jnp.bfloat16),
        jnp.asarray(spread_in(), jnp.bfloat16),
        jnp.asarray(spread_out(), jnp.bfloat16),
        jnp.broadcast_to(bias_in[None, :, None], (2, 8, 256)).reshape(16, 256),
        at,
    )
    pieces = pl.pallas_call(
        volume_kernel,
        out_shape=jax.ShapeDtypeStruct((16, 36, 128), jnp.bfloat16),
        in_specs=[VMEM] * 4 + [SMEM],
        out_specs=VMEM,
        scratch_shapes=[
            pltpu.VMEM((3, 80, 128), jnp.float32),
            pltpu.VMEM((16, 40, 128), jnp.float32),
        ],
        compiler_params=pltpu.CompilerParams(vmem_limit_bytes=16 << 20),
        cost_estimate=pl.CostEstimate(flops=1 << 26, bytes_accessed=1 << 20, transcendentals=0),
    )(far, b, near, wide, y_half)
    pieces = lax.all_to_all(pieces, "src", 0, 0, tiled=True)
    out = call(
        consensus_kernel,
        jax.ShapeDtypeStruct((64, 128), jnp.float32),
        [
            pltpu.VMEM((16, 36, 128), jnp.float32),
            pltpu.VMEM((1456, 256), jnp.bfloat16),
            pltpu.VMEM((720, 128), jnp.float32),
        ],
        1 << 28,
        pieces,
        w1,
        w2,
    )
    return out.reshape(2, 2, 16, 128)


def solution(mesh):
    mesh = jax.sharding.Mesh(mesh.devices.reshape(16, 8, 2), ("src", "z", "yh"))
    tgt = ("z", "yh")
    in_specs = (P("src", tgt, None), P(tgt, "src", None), P(), P(), P())
    out_specs = P(tgt, "src", None, None)
    return jax.shard_map(
        per_device, mesh=mesh, in_specs=in_specs, out_specs=out_specs, check_vma=False
    )
```

```python
import jax
import jax.numpy as jnp
import numpy as np
from jax import lax
from jax.experimental import pallas as pl
from jax.experimental.pallas import tpu as pltpu
from jax.sharding import PartitionSpec as P


SHIFTS = (-1, 0, 1)


def mirror_matrix():
    out = np.zeros((81, 81), np.float32)
    for p, q, r, s in np.ndindex(3, 3, 3, 3):
        out[27 * r + 9 * s + 3 * p + q, 27 * p + 9 * q + 3 * r + s] = 1
    return out


def spread_in():
    out = np.zeros((81, 2, 4, 256), np.float32)
    for k2, l, p, q, r, s in np.ndindex(2, 4, 3, 3, 3, 3):
        k, c = k2 + p, l + q
        column = r * 80 + s * 24 + k // 2 * 12 + c // 2 * 4 + k % 2 * 2 + c % 2
        out[27 * p + 9 * q + 3 * r + s, k2, l, column] = 1
    return out.reshape(81, 2048)


def spread_out():
    out = np.zeros((81, 4, 4, 128), np.float32)
    for k2, l2, p, q, r, s in np.ndindex(2, 2, 3, 3, 3, 3):
        out[27 * p + 9 * q + 3 * r + s, k2 + p, l2 + q, (r * 3 + s) * 4 + k2 * 2 + l2] = 1
    return out.reshape(81, 2048)


def shifted(x, s):
    if s == 0:
        return x
    lane = lax.broadcasted_iota(jnp.int32, x.shape, 1)
    rolled = pltpu.roll(x, (-s) % 128, 1)
    return jnp.where(lane == (127 if s == 1 else 0), 0.0, rolled)


def weights_kernel(
    cin_ref, cout_ref, mirror_ref, sel1_ref, sel2_ref, bias_ref, at_ref, w1_ref, w2_ref
):
    def parts(x):
        high = x.astype(jnp.bfloat16)
        low = (x - high.astype(jnp.float32)).astype(jnp.bfloat16)
        rows = []
        for part in (high, low):
            rows.append(part.astype(jnp.float32))
            rows.append(jnp.dot(part, mirror_ref[...], preferred_element_type=jnp.float32))
        return jnp.concatenate(rows, axis=0).astype(jnp.bfloat16)

    t1 = jnp.dot(parts(cin_ref[...]), sel1_ref[...], preferred_element_type=jnp.float32)
    lane = lax.broadcasted_iota(jnp.int32, (16, 256), 1)
    bias = bias_ref[...]
    high = bias.astype(jnp.bfloat16).astype(jnp.float32)
    for hl, part in enumerate((high, bias - high)):
        for kl in range(8):
            block = t1[hl * 16 : hl * 16 + 16, kl * 256 : kl * 256 + 256]
            for half in range(2):
                row, column = at_ref[0] + half * 2 + kl // 4, at_ref[1] + kl % 4
                inside = (row >= 0) & (row < 32) & (column >= 0) & (column < 32)
                block = jnp.where(
                    lane == 152 + half, jnp.where(inside, part, -1e30 if hl == 0 else 0.0), block
                )
            row = hl * 128 + kl * 16
            w1_ref[row : row + 16, :] = block.astype(jnp.bfloat16)
    t2 = jnp.dot(parts(cout_ref[...]), sel2_ref[...], preferred_element_type=jnp.float32)
    rows = []
    for hl in range(2):
        tall = jnp.concatenate(
            [t2[hl * 16 : hl * 16 + 16, kl * 128 : kl * 128 + 128] for kl in range(16)], axis=0
        )
        rows.append(tall.T[:40])
    w2_ref[...] = jnp.concatenate(rows, axis=0).astype(jnp.bfloat16)


def store_copies(source, target, sems):
    stores = [
        pltpu.make_async_copy(source, target.at[n], sems.at[n]) for n in range(target.shape[0])
    ]
    for store in stores:
        store.start()
    for store in stores:
        store.wait()


def b_copies_kernel(b_ref, o_ref, out_sem):
    store_copies(b_ref, o_ref, out_sem)


def a_copies_kernel(mine_ref, other_ref, y_ref, o_ref, v_ref, out_sem):
    first = y_ref[0] == 0
    mine, other = mine_ref[...], other_ref[...]
    v_ref[0] = jnp.where(first, mine, other)
    v_ref[1] = jnp.where(first, other, mine)
    store_copies(v_ref, o_ref, out_sem)


def volume_kernel(halo_ref, own_ref, swap_ref, a_ref, slot_ref, o_ref, scr_ref, tmp_ref):
    tall = jnp.concatenate([halo_ref[...], own_ref[...], swap_ref[...]], axis=0)
    scores = lax.dot_general(
        tall, a_ref[...], (((1,), (1,)), ((), ())), preferred_element_type=jnp.float32
    ) * (1024 ** -0.5)
    zeros = jnp.zeros((8, 128), jnp.float32)
    first = 2 * slot_ref[0]
    for n, slot in enumerate((first, 1, 2 - first)):
        scr_ref[slot, 0:8, :] = zeros
        scr_ref[slot, 8:72, :] = scores[64 * n : 64 * n + 64]
        scr_ref[slot, 72:80, :] = zeros
    for s in range(16):
        for n in range(3):
            tmp_ref[s, 12 * n : 12 * n + 12, :] = scr_ref[n, 4 + 4 * s : 16 + 4 * s, :]
        o_ref[s] = tmp_ref[s, 0:36, :].astype(jnp.bfloat16)


def consensus_kernel(r_ref, w1_ref, w2_ref, o_ref, rf_ref, xs_ref, ps_ref):
    xs_ref[0:80, :] = jnp.zeros((80, 256), jnp.bfloat16)
    xs_ref[1360:1456, :] = jnp.zeros((96, 256), jnp.bfloat16)
    sublane = lax.broadcasted_iota(jnp.int32, (8, 128), 0)
    for i in range(16):
        rf_ref[i] = r_ref[i].astype(jnp.float32)
        for half in range(2):
            rows = [rf_ref[i, pl.ds(half * 12 + d, 8), :] for d in range(0, 24, 8)]
            rows = [shifted(x, s) for s in SHIFTS for x in rows]
            rows.append(jnp.where(sublane == half, 1.0, 0.0))
            xs_ref[80 * (i + 1) : 80 * (i + 2), half * 128 : half * 128 + 128] = jnp.concatenate(
                rows, axis=0
            ).astype(jnp.bfloat16)
    ps_ref[0:40, :] = jnp.zeros((40, 128), jnp.float32)
    ps_ref[680:720, :] = jnp.zeros((40, 128), jnp.float32)

    def second(i, highs, lows):
        both = jnp.dot(
            w2_ref[...], jnp.concatenate(highs, axis=1), preferred_element_type=jnp.float32
        )
        more = jnp.dot(
            w2_ref[0:40, :], jnp.concatenate(lows, axis=1), preferred_element_type=jnp.float32
        )
        total = both[:40] + both[40:] + more
        ps_ref[40 * (i + 1) : 40 * (i + 2), :] = total[:, :128]
        ps_ref[40 * (i + 2) : 40 * (i + 3), :] = total[:, 128:]

    def first(i):
        rhs = xs_ref[80 * i : 80 * i + 256, :]
        return jnp.dot(w1_ref[...], rhs, preferred_element_type=jnp.float32)

    def split(acc):
        acc = acc[:128] + acc[128:]
        hidden = jnp.maximum(jnp.concatenate([acc[:, :128], acc[:, 128:]], axis=0), 0.0)
        high = hidden.astype(jnp.bfloat16)
        return high, (hidden - high.astype(jnp.float32)).astype(jnp.bfloat16)

    done = None
    for i in range(0, 16, 2):
        sums = [first(i), first(i + 1)]
        if done is not None:
            second(i - 2, *done)
        done = tuple(zip(*[split(x) for x in sums]))
    second(14, *done)
    for kl in range(4):
        out = None
        for n, s in enumerate(SHIFTS):
            part = None
            for r in range(3):
                rows = ps_ref[pl.ds(40 * r + (r * 3 + n) * 4 + kl, 16, stride=40), :]
                part = rows if part is None else part + rows
            part = shifted(part, s)
            out = part if out is None else out + part
        o_ref[kl * 16 : kl * 16 + 16, :] = out


VMEM = pl.BlockSpec(memory_space=pltpu.VMEM)
SMEM = pl.BlockSpec(memory_space=pltpu.SMEM)
HBM = pl.BlockSpec(memory_space=pltpu.HBM)


def call(kernel, outs, scratch, flops, *args):
    return pl.pallas_call(
        kernel,
        out_shape=outs,
        in_specs=[VMEM] * len(args),
        out_specs=jax.tree.map(lambda _: VMEM, outs),
        scratch_shapes=scratch,
        compiler_params=pltpu.CompilerParams(vmem_limit_bytes=16 << 20),
        cost_estimate=pl.CostEstimate(flops=flops, bytes_accessed=1 << 20, transcendentals=0),
    )(*args)


def per_device(feature_a, feature_b, conv_in, bias_in, conv_out):
    y_half = lax.axis_index("yh").reshape(1)
    b = pl.pallas_call(
        b_copies_kernel,
        out_shape=jax.ShapeDtypeStruct((16, 2, 2, 1024), jnp.bfloat16),
        in_specs=[VMEM],
        out_specs=HBM,
        scratch_shapes=[pltpu.SemaphoreType.DMA((16,))],
        compiler_params=pltpu.CompilerParams(vmem_limit_bytes=16 << 20),
    )(feature_b)
    b = lax.all_to_all(b, "src", 0, 0, tiled=True)
    b = b.reshape(64, 1024)
    other = lax.ppermute(feature_a, "yh", [(0, 1), (1, 0)])
    wide = pl.pallas_call(
        a_copies_kernel,
        out_shape=jax.ShapeDtypeStruct((8, 2, 8, 1024), jnp.bfloat16),
        in_specs=[VMEM, VMEM, SMEM],
        out_specs=HBM,
        scratch_shapes=[
            pltpu.VMEM((2, 8, 1024), jnp.bfloat16),
            pltpu.SemaphoreType.DMA((8,)),
        ],
        compiler_params=pltpu.CompilerParams(vmem_limit_bytes=16 << 20),
    )(feature_a[0], other[0], y_half)
    wide = lax.all_to_all(wide, "z", 0, 0, tiled=True)
    wide = wide.reshape(128, 1024)
    place = ("src", "z", "yh")
    pairs = []
    for index in range(0, 256, 16):
        if index // 16 % 2:
            pairs += [(index + t, index + (t ^ 1)) for t in range(16)]
        else:
            pairs += [(index + t, index + ((t - 1) ^ 1) + 1) for t in range(1, 15)]
    halo = lax.ppermute(b, place, pairs)
    swapped = lax.ppermute(halo, place, [(n, n ^ 16) for n in range(256)])
    slot = (lax.axis_index("src") % 2) ^ lax.axis_index("yh")
    at = jnp.stack([lax.axis_index(("z", "yh")) * 2 - 1, lax.axis_index("src") * 2 - 1])
    w1, w2 = pl.pallas_call(
        weights_kernel,
        out_shape=(
            jax.ShapeDtypeStruct((256, 256), jnp.bfloat16),
            jax.ShapeDtypeStruct((80, 256), jnp.bfloat16),
        ),
        in_specs=[VMEM] * 6 + [SMEM],
        out_specs=(VMEM,) * 2,
        compiler_params=pltpu.CompilerParams(vmem_limit_bytes=16 << 20),
        cost_estimate=pl.CostEstimate(
            flops=1 << 24, bytes_accessed=1 << 20, transcendentals=0
        ),
    )(
        conv_in,
        conv_out,
        jnp.asarray(mirror_matrix(), jnp.bfloat16),
        jnp.asarray(spread_in(), jnp.bfloat16),
        jnp.asarray(spread_out(), jnp.bfloat16),
        jnp.broadcast_to(bias_in[None, :, None], (2, 8, 256)).reshape(16, 256),
        at,
    )
    pieces = pl.pallas_call(
        volume_kernel,
        out_shape=jax.ShapeDtypeStruct((16, 36, 128), jnp.bfloat16),
        in_specs=[VMEM] * 4 + [SMEM],
        out_specs=VMEM,
        scratch_shapes=[
            pltpu.VMEM((3, 80, 128), jnp.float32),
            pltpu.VMEM((16, 40, 128), jnp.float32),
        ],
        compiler_params=pltpu.CompilerParams(vmem_limit_bytes=16 << 20),
        cost_estimate=pl.CostEstimate(flops=1 << 26, bytes_accessed=1 << 20, transcendentals=0),
    )(halo, b, swapped, wide, slot.reshape(1))
    pieces = lax.all_to_all(pieces, "src", 0, 0, tiled=True)
    out = call(
        consensus_kernel,
        jax.ShapeDtypeStruct((64, 128), jnp.float32),
        [
            pltpu.VMEM((16, 36, 128), jnp.float32),
            pltpu.VMEM((1456, 256), jnp.bfloat16),
            pltpu.VMEM((720, 128), jnp.float32),
        ],
        1 << 28,
        pieces,
        w1,
        w2,
    )
    return out.reshape(2, 2, 16, 128)


def solution(mesh):
    mesh = jax.sharding.Mesh(mesh.devices.reshape(16, 8, 2), ("src", "z", "yh"))
    tgt = ("z", "yh")
    in_specs = (P("src", tgt, None), P(tgt, "src", None), P(), P(), P())
    out_specs = P(tgt, "src", None, None)
    return jax.shard_map(
        per_device, mesh=mesh, in_specs=in_specs, out_specs=out_specs, check_vma=False
    )
```

```python
import jax
import jax.numpy as jnp
import numpy as np
from jax import lax
from jax.experimental import pallas as pl
from jax.experimental.pallas import tpu as pltpu
from jax.sharding import PartitionSpec as P


SHIFTS = (-1, 0, 1)


def mirror_matrix():
    out = np.zeros((81, 81), np.float32)
    for p, q, r, s in np.ndindex(3, 3, 3, 3):
        out[27 * r + 9 * s + 3 * p + q, 27 * p + 9 * q + 3 * r + s] = 1
    return out


def spread_in():
    out = np.zeros((81, 2, 4, 256), np.float32)
    for k2, l, p, q, r, s in np.ndindex(2, 4, 3, 3, 3, 3):
        k, c = k2 + p, l + q
        column = r * 80 + s * 24 + k // 2 * 12 + c // 2 * 4 + k % 2 * 2 + c % 2
        out[27 * p + 9 * q + 3 * r + s, k2, l, column] = 1
    return out.reshape(81, 2048)


def spread_out():
    out = np.zeros((81, 4, 4, 128), np.float32)
    for k2, l2, p, q, r, s in np.ndindex(2, 2, 3, 3, 3, 3):
        out[27 * p + 9 * q + 3 * r + s, k2 + p, l2 + q, (r * 3 + s) * 4 + k2 * 2 + l2] = 1
    return out.reshape(81, 2048)


def shifted(x, s):
    if s == 0:
        return x
    lane = lax.broadcasted_iota(jnp.int32, x.shape, 1)
    rolled = pltpu.roll(x, (-s) % 128, 1)
    return jnp.where(lane == (127 if s == 1 else 0), 0.0, rolled)


def weights_kernel(
    cin_ref, cout_ref, mirror_ref, sel1_ref, sel2_ref, bias_ref, at_ref, w1_ref, w2_ref
):
    def parts(x):
        high = x.astype(jnp.bfloat16)
        low = (x - high.astype(jnp.float32)).astype(jnp.bfloat16)
        rows = []
        for part in (high, low):
            rows.append(part.astype(jnp.float32))
            rows.append(jnp.dot(part, mirror_ref[...], preferred_element_type=jnp.float32))
        return jnp.concatenate(rows, axis=0).astype(jnp.bfloat16)

    t1 = jnp.dot(parts(cin_ref[...]), sel1_ref[...], preferred_element_type=jnp.float32)
    lane = lax.broadcasted_iota(jnp.int32, (16, 256), 1)
    bias = bias_ref[...]
    high = bias.astype(jnp.bfloat16).astype(jnp.float32)
    for hl, part in enumerate((high, bias - high)):
        for kl in range(8):
            block = t1[hl * 16 : hl * 16 + 16, kl * 256 : kl * 256 + 256]
            for half in range(2):
                row, column = at_ref[0] + half * 2 + kl // 4, at_ref[1] + kl % 4
                inside = (row >= 0) & (row < 32) & (column >= 0) & (column < 32)
                block = jnp.where(
                    lane == 152 + half, jnp.where(inside, part, -1e30 if hl == 0 else 0.0), block
                )
            row = hl * 128 + kl * 16
            w1_ref[row : row + 16, :] = block.astype(jnp.bfloat16)
    t2 = jnp.dot(parts(cout_ref[...]), sel2_ref[...], preferred_element_type=jnp.float32)
    rows = []
    for hl in range(2):
        tall = jnp.concatenate(
            [t2[hl * 16 : hl * 16 + 16, kl * 128 : kl * 128 + 128] for kl in range(16)], axis=0
        )
        rows.append(tall.T[:40])
    w2_ref[...] = jnp.concatenate(rows, axis=0).astype(jnp.bfloat16)


def b_copies_kernel(b_ref, o_ref):
    for n in range(o_ref.shape[0]):
        o_ref[n] = b_ref[...]


def a_copies_kernel(mine_ref, other_ref, y_ref, o_ref):
    first = y_ref[0] == 0
    mine, other = mine_ref[...], other_ref[...]
    low, high = jnp.where(first, mine, other), jnp.where(first, other, mine)
    for n in range(o_ref.shape[0]):
        o_ref[n, 0] = low
        o_ref[n, 1] = high


def volume_kernel(halo_ref, own_ref, swap_ref, a_ref, slot_ref, o_ref, scr_ref, tmp_ref):
    tall = jnp.concatenate([halo_ref[...], own_ref[...], swap_ref[...]], axis=0)
    scores = lax.dot_general(
        tall, a_ref[...], (((1,), (1,)), ((), ())), preferred_element_type=jnp.float32
    ) * (1024 ** -0.5)
    zeros = jnp.zeros((8, 128), jnp.float32)
    first = 2 * slot_ref[0]
    for n, slot in enumerate((first, 1, 2 - first)):
        scr_ref[slot, 0:8, :] = zeros
        scr_ref[slot, 8:72, :] = scores[64 * n : 64 * n + 64]
        scr_ref[slot, 72:80, :] = zeros
    for s in range(16):
        for n in range(3):
            tmp_ref[s, 12 * n : 12 * n + 12, :] = scr_ref[n, 4 + 4 * s : 16 + 4 * s, :]
        o_ref[s] = tmp_ref[s, 0:36, :].astype(jnp.bfloat16)


def consensus_kernel(r_ref, w1_ref, w2_ref, y_ref, o_ref, rf_ref, xs_ref, ps_ref):
    xs_ref[0:80, :] = jnp.zeros((80, 256), jnp.bfloat16)
    xs_ref[1360:1456, :] = jnp.zeros((96, 256), jnp.bfloat16)
    sublane = lax.broadcasted_iota(jnp.int32, (8, 128), 0)
    mine = ((lax.broadcasted_iota(jnp.int32, (36, 128), 1) >> 3) & 1) == y_ref[0]
    for i in range(16):
        rf_ref[i] = jnp.where(mine, r_ref[i].astype(jnp.float32), r_ref[i ^ 8].astype(jnp.float32))
        for half in range(2):
            rows = [rf_ref[i, pl.ds(half * 12 + d, 8), :] for d in range(0, 24, 8)]
            rows = [shifted(x, s) for s in SHIFTS for x in rows]
            rows.append(jnp.where(sublane == half, 1.0, 0.0))
            xs_ref[80 * (i + 1) : 80 * (i + 2), half * 128 : half * 128 + 128] = jnp.concatenate(
                rows, axis=0
            ).astype(jnp.bfloat16)
    ps_ref[0:40, :] = jnp.zeros((40, 128), jnp.float32)
    ps_ref[680:720, :] = jnp.zeros((40, 128), jnp.float32)

    def second(i, highs, lows):
        both = jnp.dot(
            w2_ref[...], jnp.concatenate(highs, axis=1), preferred_element_type=jnp.float32
        )
        more = jnp.dot(
            w2_ref[0:40, :], jnp.concatenate(lows, axis=1), preferred_element_type=jnp.float32
        )
        total = both[:40] + both[40:] + more
        ps_ref[40 * (i + 1) : 40 * (i + 2), :] = total[:, :128]
        ps_ref[40 * (i + 2) : 40 * (i + 3), :] = total[:, 128:]

    def first(i):
        rhs = xs_ref[80 * i : 80 * i + 256, :]
        return jnp.dot(w1_ref[...], rhs, preferred_element_type=jnp.float32)

    def split(acc):
        acc = acc[:128] + acc[128:]
        hidden = jnp.maximum(jnp.concatenate([acc[:, :128], acc[:, 128:]], axis=0), 0.0)
        high = hidden.astype(jnp.bfloat16)
        return high, (hidden - high.astype(jnp.float32)).astype(jnp.bfloat16)

    done = None
    for i in range(0, 16, 2):
        sums = [first(i), first(i + 1)]
        if done is not None:
            second(i - 2, *done)
        done = tuple(zip(*[split(x) for x in sums]))
    second(14, *done)
    for kl in range(4):
        out = None
        for n, s in enumerate(SHIFTS):
            part = None
            for r in range(3):
                rows = ps_ref[pl.ds(40 * r + (r * 3 + n) * 4 + kl, 16, stride=40), :]
                part = rows if part is None else part + rows
            part = shifted(part, s)
            out = part if out is None else out + part
        o_ref[kl * 16 : kl * 16 + 16, :] = out


VMEM = pl.BlockSpec(memory_space=pltpu.VMEM)
SMEM = pl.BlockSpec(memory_space=pltpu.SMEM)


def per_device(feature_a, feature_b, conv_in, bias_in, conv_out):
    y_half = lax.axis_index("yh").reshape(1)
    b = pl.pallas_call(
        b_copies_kernel,
        out_shape=jax.ShapeDtypeStruct((16, 2, 2, 1024), jnp.bfloat16),
        in_specs=[VMEM],
        out_specs=VMEM,
        compiler_params=pltpu.CompilerParams(vmem_limit_bytes=16 << 20),
    )(feature_b)
    b = lax.all_to_all(b, "src", 0, 0, tiled=True)
    b = b.reshape(64, 1024)
    other = lax.ppermute(
        feature_a, ("src", "z", "yh"), [(n, n ^ 129) for n in range(256)]
    )
    wide = pl.pallas_call(
        a_copies_kernel,
        out_shape=jax.ShapeDtypeStruct((8, 2, 8, 1024), jnp.bfloat16),
        in_specs=[VMEM, VMEM, SMEM],
        out_specs=VMEM,
        compiler_params=pltpu.CompilerParams(vmem_limit_bytes=16 << 20),
    )(feature_a[0], other[0], y_half)
    wide = lax.all_to_all(wide, "z", 0, 0, tiled=True)
    wide = wide.reshape(128, 1024)
    place = ("src", "z", "yh")
    pairs = []
    for index in range(0, 256, 16):
        if index // 16 % 2:
            pairs += [(index + t, index + (t ^ 1)) for t in range(16)]
        else:
            pairs += [(index + t, index + ((t - 1) ^ 1) + 1) for t in range(1, 15)]
    halo = lax.ppermute(b, place, pairs)
    swapped = lax.ppermute(halo, place, [(n, n ^ 16) for n in range(256)])
    slot = (lax.axis_index("src") % 2) ^ lax.axis_index("yh")
    at = jnp.stack([lax.axis_index(("z", "yh")) * 2 - 1, lax.axis_index("src") * 2 - 1])
    w1, w2 = pl.pallas_call(
        weights_kernel,
        out_shape=(
            jax.ShapeDtypeStruct((256, 256), jnp.bfloat16),
            jax.ShapeDtypeStruct((80, 256), jnp.bfloat16),
        ),
        in_specs=[VMEM] * 6 + [SMEM],
        out_specs=(VMEM,) * 2,
        compiler_params=pltpu.CompilerParams(vmem_limit_bytes=16 << 20),
        cost_estimate=pl.CostEstimate(
            flops=1 << 24, bytes_accessed=1 << 20, transcendentals=0
        ),
    )(
        conv_in,
        conv_out,
        jnp.asarray(mirror_matrix(), jnp.bfloat16),
        jnp.asarray(spread_in(), jnp.bfloat16),
        jnp.asarray(spread_out(), jnp.bfloat16),
        jnp.broadcast_to(bias_in[None, :, None], (2, 8, 256)).reshape(16, 256),
        at,
    )
    pieces = pl.pallas_call(
        volume_kernel,
        out_shape=jax.ShapeDtypeStruct((16, 36, 128), jnp.bfloat16),
        in_specs=[VMEM] * 4 + [SMEM],
        out_specs=VMEM,
        scratch_shapes=[
            pltpu.VMEM((3, 80, 128), jnp.float32),
            pltpu.VMEM((16, 40, 128), jnp.float32),
        ],
        compiler_params=pltpu.CompilerParams(vmem_limit_bytes=16 << 20),
        cost_estimate=pl.CostEstimate(flops=1 << 26, bytes_accessed=1 << 20, transcendentals=0),
    )(halo, b, swapped, wide, slot.reshape(1))
    pieces = lax.all_to_all(pieces, "src", 0, 0, tiled=True)
    out = pl.pallas_call(
        consensus_kernel,
        out_shape=jax.ShapeDtypeStruct((64, 128), jnp.float32),
        in_specs=[VMEM] * 3 + [SMEM],
        out_specs=VMEM,
        scratch_shapes=[
            pltpu.VMEM((16, 36, 128), jnp.float32),
            pltpu.VMEM((1456, 256), jnp.bfloat16),
            pltpu.VMEM((720, 128), jnp.float32),
        ],
        compiler_params=pltpu.CompilerParams(vmem_limit_bytes=16 << 20),
        cost_estimate=pl.CostEstimate(flops=1 << 28, bytes_accessed=1 << 20, transcendentals=0),
    )(pieces, w1, w2, y_half)
    return out.reshape(2, 2, 16, 128)


def solution(mesh):
    mesh = jax.sharding.Mesh(mesh.devices.reshape(16, 8, 2), ("src", "z", "yh"))
    tgt = ("z", "yh")
    in_specs = (P("src", tgt, None), P(tgt, "src", None), P(), P(), P())
    out_specs = P(tgt, "src", None, None)
    return jax.shard_map(
        per_device, mesh=mesh, in_specs=in_specs, out_specs=out_specs, check_vma=False
    )
```

```python
import jax
import jax.numpy as jnp
import numpy as np
from jax import lax
from jax.experimental import pallas as pl
from jax.experimental.pallas import tpu as pltpu
from jax.sharding import PartitionSpec as P


SHIFTS = (-1, 0, 1)


def mirror_matrix():
    out = np.zeros((81, 81), np.float32)
    for p, q, r, s in np.ndindex(3, 3, 3, 3):
        out[27 * r + 9 * s + 3 * p + q, 27 * p + 9 * q + 3 * r + s] = 1
    return out


def spread_in():
    out = np.zeros((81, 2, 4, 256), np.float32)
    for k2, l, p, q, r, s in np.ndindex(2, 4, 3, 3, 3, 3):
        k, c = k2 + p, l + q
        column = r * 80 + s * 24 + k // 2 * 12 + c // 2 * 4 + k % 2 * 2 + c % 2
        out[27 * p + 9 * q + 3 * r + s, k2, l, column] = 1
    return out.reshape(81, 2048)


def spread_out():
    out = np.zeros((81, 4, 4, 128), np.float32)
    for k2, l2, p, q, r, s in np.ndindex(2, 2, 3, 3, 3, 3):
        out[27 * p + 9 * q + 3 * r + s, k2 + p, l2 + q, (r * 3 + s) * 4 + k2 * 2 + l2] = 1
    return out.reshape(81, 2048)


def shifted(x, s):
    if s == 0:
        return x
    lane = lax.broadcasted_iota(jnp.int32, x.shape, 1)
    rolled = pltpu.roll(x, (-s) % 128, 1)
    return jnp.where(lane == (127 if s == 1 else 0), 0.0, rolled)


def weights_kernel(
    cin_ref, cout_ref, mirror_ref, sel1_ref, sel2_ref, bias_ref, at_ref, w1_ref, w2_ref
):
    def parts(x):
        high = x.astype(jnp.bfloat16)
        low = (x - high.astype(jnp.float32)).astype(jnp.bfloat16)
        rows = []
        for part in (high, low):
            rows.append(part.astype(jnp.float32))
            rows.append(jnp.dot(part, mirror_ref[...], preferred_element_type=jnp.float32))
        return jnp.concatenate(rows, axis=0).astype(jnp.bfloat16)

    t1 = jnp.dot(parts(cin_ref[...]), sel1_ref[...], preferred_element_type=jnp.float32)
    lane = lax.broadcasted_iota(jnp.int32, (16, 256), 1)
    bias = bias_ref[...]
    high = bias.astype(jnp.bfloat16).astype(jnp.float32)
    for hl, part in enumerate((high, bias - high)):
        for kl in range(8):
            block = t1[hl * 16 : hl * 16 + 16, kl * 256 : kl * 256 + 256]
            for half in range(2):
                row, column = at_ref[0] + half * 2 + kl // 4, at_ref[1] + kl % 4
                inside = (row >= 0) & (row < 32) & (column >= 0) & (column < 32)
                block = jnp.where(
                    lane == 152 + half, jnp.where(inside, part, -1e30 if hl == 0 else 0.0), block
                )
            row = hl * 128 + kl * 16
            w1_ref[row : row + 16, :] = block.astype(jnp.bfloat16)
    t2 = jnp.dot(parts(cout_ref[...]), sel2_ref[...], preferred_element_type=jnp.float32)
    rows = []
    for hl in range(2):
        tall = jnp.concatenate(
            [t2[hl * 16 : hl * 16 + 16, kl * 128 : kl * 128 + 128] for kl in range(16)], axis=0
        )
        rows.append(tall.T[:40])
    w2_ref[...] = jnp.concatenate(rows, axis=0).astype(jnp.bfloat16)


def b_copies_kernel(b_ref, o_ref):
    for n in range(o_ref.shape[0]):
        o_ref[n] = b_ref[...]


def a_copies_kernel(mine_ref, other_ref, y_ref, o_ref):
    first = y_ref[0] == 0
    mine, other = mine_ref[...], other_ref[...]
    low, high = jnp.where(first, mine, other), jnp.where(first, other, mine)
    for n in range(o_ref.shape[0]):
        o_ref[n, 0] = low
        o_ref[n, 1] = high


def volume_kernel(halo_ref, own_ref, swap_ref, a_ref, slot_ref, o_ref, scr_ref, tmp_ref):
    tall = jnp.concatenate([halo_ref[...], own_ref[...], swap_ref[...]], axis=0)
    scores = lax.dot_general(
        tall, a_ref[...], (((1,), (1,)), ((), ())), preferred_element_type=jnp.float32
    ) * (1024 ** -0.5)
    zeros = jnp.zeros((8, 128), jnp.float32)
    first = 2 * slot_ref[0]
    for n, slot in enumerate((first, 1, 2 - first)):
        scr_ref[slot, 0:8, :] = zeros
        scr_ref[slot, 8:72, :] = scores[64 * n : 64 * n + 64]
        scr_ref[slot, 72:80, :] = zeros
    for s in range(16):
        for n in range(3):
            tmp_ref[s, 12 * n : 12 * n + 12, :] = scr_ref[n, 4 + 4 * s : 16 + 4 * s, :]
        o_ref[s] = tmp_ref[s, 0:36, :].astype(jnp.bfloat16)


def consensus_kernel(r_ref, w1_ref, w2_ref, y_ref, o_ref, rf_ref, xs_ref, ps_ref):
    xs_ref[0:80, :] = jnp.zeros((80, 256), jnp.bfloat16)
    xs_ref[1360:1456, :] = jnp.zeros((96, 256), jnp.bfloat16)
    sublane = lax.broadcasted_iota(jnp.int32, (8, 128), 0)
    mine = ((lax.broadcasted_iota(jnp.int32, (36, 128), 1) >> 3) & 1) == y_ref[0]
    for i in range(16):
        rf_ref[i] = jnp.where(mine, r_ref[i], r_ref[i ^ 8]).astype(jnp.float32)
        for half in range(2):
            rows = [rf_ref[i, pl.ds(half * 12 + d, 8), :] for d in range(0, 24, 8)]
            rows = [shifted(x, s) for s in SHIFTS for x in rows]
            rows.append(jnp.where(sublane == half, 1.0, 0.0))
            xs_ref[80 * (i + 1) : 80 * (i + 2), half * 128 : half * 128 + 128] = jnp.concatenate(
                rows, axis=0
            ).astype(jnp.bfloat16)
    ps_ref[0:40, :] = jnp.zeros((40, 128), jnp.float32)
    ps_ref[680:720, :] = jnp.zeros((40, 128), jnp.float32)

    def second(i, highs, lows):
        both = jnp.dot(
            w2_ref[...], jnp.concatenate(highs, axis=1), preferred_element_type=jnp.float32
        )
        more = jnp.dot(
            w2_ref[0:40, :], jnp.concatenate(lows, axis=1), preferred_element_type=jnp.float32
        )
        total = both[:40] + both[40:] + more
        ps_ref[40 * (i + 1) : 40 * (i + 2), :] = total[:, :128]
        ps_ref[40 * (i + 2) : 40 * (i + 3), :] = total[:, 128:]

    def first(i):
        rhs = xs_ref[80 * i : 80 * i + 256, :]
        return jnp.dot(w1_ref[...], rhs, preferred_element_type=jnp.float32)

    def split(acc):
        acc = acc[:128] + acc[128:]
        hidden = jnp.maximum(jnp.concatenate([acc[:, :128], acc[:, 128:]], axis=0), 0.0)
        high = hidden.astype(jnp.bfloat16)
        return high, (hidden - high.astype(jnp.float32)).astype(jnp.bfloat16)

    done = None
    for i in range(0, 16, 2):
        sums = [first(i), first(i + 1)]
        if done is not None:
            second(i - 2, *done)
        done = tuple(zip(*[split(x) for x in sums]))
    second(14, *done)
    for kl in range(4):
        out = None
        for n, s in enumerate(SHIFTS):
            part = None
            for r in range(3):
                rows = ps_ref[pl.ds(40 * r + (r * 3 + n) * 4 + kl, 16, stride=40), :]
                part = rows if part is None else part + rows
            part = shifted(part, s)
            out = part if out is None else out + part
        o_ref[kl * 16 : kl * 16 + 16, :] = out


VMEM = pl.BlockSpec(memory_space=pltpu.VMEM)
SMEM = pl.BlockSpec(memory_space=pltpu.SMEM)


def per_device(feature_a, feature_b, conv_in, bias_in, conv_out):
    y_half = lax.axis_index("yh").reshape(1)
    b = pl.pallas_call(
        b_copies_kernel,
        out_shape=jax.ShapeDtypeStruct((16, 2, 2, 1024), jnp.bfloat16),
        in_specs=[VMEM],
        out_specs=VMEM,
        compiler_params=pltpu.CompilerParams(vmem_limit_bytes=16 << 20),
    )(feature_b)
    b = lax.all_to_all(b, "src", 0, 0, tiled=True)
    b = b.reshape(64, 1024)
    other = lax.ppermute(
        feature_a, ("src", "z", "yh"), [(n, n ^ 129) for n in range(256)]
    )
    wide = pl.pallas_call(
        a_copies_kernel,
        out_shape=jax.ShapeDtypeStruct((8, 2, 8, 1024), jnp.bfloat16),
        in_specs=[VMEM, VMEM, SMEM],
        out_specs=VMEM,
        compiler_params=pltpu.CompilerParams(vmem_limit_bytes=16 << 20),
    )(feature_a[0], other[0], y_half)
    wide = lax.all_to_all(wide, "z", 0, 0, tiled=True)
    wide = wide.reshape(128, 1024)
    place = ("src", "z", "yh")
    pairs = []
    for index in range(0, 256, 16):
        if index // 16 % 2:
            pairs += [(index + t, (index ^ 128) + (t ^ 1)) for t in range(16)]
        else:
            pairs += [(index + t, (index ^ 128) + ((t - 1) ^ 1) + 1) for t in range(1, 15)]
    halo = lax.ppermute(b, place, pairs)
    swapped = lax.ppermute(halo, place, [(n, n ^ 16) for n in range(256)])
    slot = (lax.axis_index("src") % 2) ^ lax.axis_index("yh")
    at = jnp.stack([lax.axis_index(("z", "yh")) * 2 - 1, lax.axis_index("src") * 2 - 1])
    w1, w2 = pl.pallas_call(
        weights_kernel,
        out_shape=(
            jax.ShapeDtypeStruct((256, 256), jnp.bfloat16),
            jax.ShapeDtypeStruct((80, 256), jnp.bfloat16),
        ),
        in_specs=[VMEM] * 6 + [SMEM],
        out_specs=(VMEM,) * 2,
        compiler_params=pltpu.CompilerParams(vmem_limit_bytes=16 << 20),
        cost_estimate=pl.CostEstimate(
            flops=1 << 24, bytes_accessed=1 << 20, transcendentals=0
        ),
    )(
        conv_in,
        conv_out,
        jnp.asarray(mirror_matrix(), jnp.bfloat16),
        jnp.asarray(spread_in(), jnp.bfloat16),
        jnp.asarray(spread_out(), jnp.bfloat16),
        jnp.broadcast_to(bias_in[None, :, None], (2, 8, 256)).reshape(16, 256),
        at,
    )
    pieces = pl.pallas_call(
        volume_kernel,
        out_shape=jax.ShapeDtypeStruct((16, 36, 128), jnp.bfloat16),
        in_specs=[VMEM] * 4 + [SMEM],
        out_specs=VMEM,
        scratch_shapes=[
            pltpu.VMEM((3, 80, 128), jnp.float32),
            pltpu.VMEM((16, 40, 128), jnp.float32),
        ],
        compiler_params=pltpu.CompilerParams(vmem_limit_bytes=16 << 20),
        cost_estimate=pl.CostEstimate(flops=1 << 26, bytes_accessed=1 << 20, transcendentals=0),
    )(halo, b, swapped, wide, slot.reshape(1))
    pieces = lax.all_to_all(pieces, "src", 0, 0, tiled=True)
    out = pl.pallas_call(
        consensus_kernel,
        out_shape=jax.ShapeDtypeStruct((64, 128), jnp.float32),
        in_specs=[VMEM] * 3 + [SMEM],
        out_specs=VMEM,
        scratch_shapes=[
            pltpu.VMEM((16, 36, 128), jnp.float32),
            pltpu.VMEM((1456, 256), jnp.bfloat16),
            pltpu.VMEM((720, 128), jnp.float32),
        ],
        compiler_params=pltpu.CompilerParams(vmem_limit_bytes=16 << 20),
        cost_estimate=pl.CostEstimate(flops=1 << 28, bytes_accessed=1 << 20, transcendentals=0),
    )(pieces, w1, w2, y_half)
    return out.reshape(2, 2, 16, 128)


def solution(mesh):
    mesh = jax.sharding.Mesh(mesh.devices.reshape(16, 8, 2), ("src", "z", "yh"))
    tgt = ("z", "yh")
    in_specs = (P("src", tgt, None), P(tgt, "src", None), P(), P(), P())
    out_specs = P(tgt, "src", None, None)
    return jax.shard_map(
        per_device, mesh=mesh, in_specs=in_specs, out_specs=out_specs, check_vma=False
    )
```
